32 devices in a mesh: fsdp: 4 (over z), ctx: 4 (over y, x), tp: 2 (over core).
Axes of the slice: x: 2, y: 2, z: 4, core: 2. Of those that a mesh axis runs over, the one named last changes fastest.
Arguments:
- hidden_in: bfloat16 [4, 2048, 1536], P('fsdp', 'ctx'), may hold values from -6 to 6
- segment_ids: int32 [4, 2048], P('fsdp', 'ctx'), may hold values from 0 to 6, as said below
- positions: int32 [4, 2048], P('fsdp', 'ctx'), may hold values from 0 to 1279, as said below
- attn_gain: bfloat16 [1536], P('fsdp'), may hold values from 0.5 to 1.5
- q_weight: bfloat16 [1536, 1536], P('fsdp', 'tp'), may hold values from -0.15625 to 0.15625
- k_weight: bfloat16 [1536, 768], P('fsdp', 'tp'), may hold values from -0.15625 to 0.15625
- v_weight: bfloat16 [1536, 768], P('fsdp', 'tp'), may hold values from -0.15625 to 0.15625
- o_weight: bfloat16 [1536, 1536], P('fsdp', 'tp'), may hold values from -3.5 to 3.5
- mlp_gain: bfloat16 [1536], P('fsdp'), may hold values from 0.5 to 1.5
- gate_weight: bfloat16 [1536, 4096], P('fsdp', 'tp'), may hold values from -0.15625 to 0.15625
- up_weight: bfloat16 [1536, 4096], P('fsdp', 'tp'), may hold values from -0.15625 to 0.15625
- down_weight: bfloat16 [1536, 4096], P('fsdp', 'tp'), may hold values from -0.09375 to 0.09375
- cotangent: bfloat16 [4, 2048, 1536], P('fsdp', 'ctx'), may hold values from -6 to 6
Outputs:
- mixed: bfloat16 [4, 2048, 1536], P('fsdp', 'ctx')
- input_grad: bfloat16 [4, 2048, 1536], P('fsdp', 'ctx')
- attn_gain_grad: float32 [1536], P('fsdp')
- q_grad: float32 [1536, 1536], P('fsdp', 'tp')
- k_grad: float32 [1536, 768], P('fsdp', 'tp')
- v_grad: float32 [1536, 768], P('fsdp', 'tp')
- o_grad: float32 [1536, 1536], P('fsdp', 'tp')
- mlp_gain_grad: float32 [1536], P('fsdp')
- gate_grad: float32 [1536, 4096], P('fsdp', 'tp')
- up_grad: float32 [1536, 4096], P('fsdp', 'tp')
- down_grad: float32 [1536, 4096], P('fsdp', 'tp')
The draws below stay inside these ranges and needn't reach their ends.
Inputs may be any that keep to these rules, and one draw needn't show every extreme that they name: `segment_ids`: within a pack the numbers start at 0, never fall and rise by one at each new document; every pack holds exactly seven documents, each of 1 to 1280 positions, one of exactly 1280. `positions`: each entry is the number of earlier positions of the same document in its pack.
All inputs are finite; a program needn't handle non-finite values.
Results may differ from the reference program's by a relative error of at most 0.025.
Values may be sent and summed in bfloat16 or wider, within the bound.
No kernel may reach another device: no remote copies, remote signals or barrier semaphores. Data moves between devices by JAX's collectives and lax.ppermute only.
A program may use at most 256 MiB of HBM per device.

```python
import math
import jax
import jax.numpy as jnp
from jax import lax

D = 1536
HQ = 16
KV = 8
HD = 96
FF = 4096
PACKS = 4
PACK_LEN = 2048
MOST = 1280
QW = 1536
KW = 768


def pack_row(row_key):
    start_key, order_key = jax.random.split(row_key)
    index_row = jnp.arange(PACK_LEN, dtype=jnp.int32)
    long_start = jax.random.randint(start_key, (), 1, PACK_LEN - MOST, dtype=jnp.int32)
    long_stop = long_start + MOST
    inside = (index_row >= long_start) & (index_row <= long_stop)
    eligible = jnp.logical_not(inside) & (index_row > 0)
    order_row = jax.random.permutation(order_key, PACK_LEN).astype(jnp.int32)
    scores = jnp.where(eligible, order_row, -1).astype(jnp.int32)
    unused, picked = lax.top_k(scores, 4)
    extra = jnp.any(index_row[:, None] == picked[None, :].astype(jnp.int32), axis=1)
    boundary = (index_row == long_start) | (index_row == long_stop) | extra
    segment_row = jnp.cumsum(boundary.astype(jnp.int32)).astype(jnp.int32)
    last_cut = lax.cummax(jnp.where(boundary, index_row, 0).astype(jnp.int32), axis=0)
    return (segment_row, (index_row - last_cut).astype(jnp.int32))


def pack_layout(key):
    base_key = jax.random.fold_in(key, 11)
    row_keys = jax.random.split(base_key, PACKS)
    return jax.vmap(pack_row)(row_keys)


def draw_segment_ids(key, part):
    return pack_layout(key)[0]


def draw_positions(key, part):
    return pack_layout(key)[1]


def with_spikes(drawn, stream_key, source, target, blocks, factor):
    def block_of(position):
        return (jnp.arange(drawn.shape[position]) // (drawn.shape[position] // blocks)).reshape((-1,) + (1,) * (drawn.ndim - 1 - position))

    one_side = jax.random.permutation(stream_key, blocks)[block_of(target)]
    other_side = (block_of(target) + blocks // 2) % blocks
    return jnp.where((block_of(source) == one_side) | (block_of(source) == other_side), factor * drawn, drawn)


def level_of(key, dims, pieces, least, largest):
    gain, own = 1.0, jax.random.fold_in(key, 6)
    for dim, shards_of in pieces:
        heights = jnp.exp(jax.random.uniform(jax.random.fold_in(own, dim), (shards_of,), jnp.float32, least / len(pieces), largest / len(pieces)))
        gain = gain * jnp.repeat(heights, dims[dim] // shards_of).reshape([-1 if axis == dim else 1 for axis in range(len(dims))])
    return gain


def gaussian(key, extent, scale, bound, shards=(), kind=jnp.bfloat16):
    level = level_of(key, extent, shards, -0.22, 0.18) if shards else 1.0
    values = jax.random.normal(key, extent, jnp.float32) * scale * level
    return jnp.minimum(jnp.maximum(values, -bound), bound).astype(kind)


def gaussian_with(rng, extent, spread, reach, pieces, heavy, held_as=jnp.bfloat16):
    drawn = spread * jax.random.normal(rng, extent, jnp.float32)
    if pieces:
        drawn = drawn * level_of(rng, extent, pieces, -0.22, 0.18)
    return jnp.clip(with_spikes(drawn, jax.random.fold_in(rng, 3), *heavy), -reach, reach).astype(held_as)


def setup_inputs(seed: int = 0) -> dict:
    arg_keys = jax.random.split(jax.random.key(seed), 14)
    hidden_in = gaussian(arg_keys[0], (PACKS, PACK_LEN, D), 1.0, 6.0, ((0, 4), (1, 4)))
    segment_ids = draw_segment_ids(jax.random.fold_in(arg_keys[13], 71), 0)
    positions = draw_positions(jax.random.fold_in(arg_keys[13], 71), 0)
    attn_gain = jnp.clip(1.0 + 0.1 * jax.random.normal(arg_keys[3], (D,), jnp.float32), 0.5, 1.5).astype(jnp.bfloat16)
    q_weight = gaussian(arg_keys[4], (D, QW), D ** -0.5, 0.15625, ((0, 4), (1, 2)))
    k_weight = gaussian(arg_keys[5], (D, KW), D ** -0.5, 0.15625, ((0, 4), (1, 2)))
    v_weight = gaussian(arg_keys[6], (D, KW), D ** -0.5, 0.15625, ((0, 4), (1, 2)))
    o_weight = gaussian(arg_keys[7], (D, QW), (max(1, QW // 512)) ** -0.5, 3.5, ((0, 4), (1, 2)))
    mlp_gain = jnp.clip(1.0 + 0.1 * jax.random.normal(arg_keys[8], (D,), jnp.float32), 0.5, 1.5).astype(jnp.bfloat16)
    gate_weight = gaussian(arg_keys[9], (D, FF), D ** -0.5, 0.15625, ((0, 4), (1, 2)))
    up_weight = gaussian(arg_keys[10], (D, FF), D ** -0.5, 0.15625, ((0, 4), (1, 2)))
    down_weight = gaussian(arg_keys[11], (D, FF), FF ** -0.5, 0.09375, ((0, 4), (1, 2)))
    cotangent = gaussian_with(arg_keys[12], (PACKS, PACK_LEN, D), 1.0, 6.0, ((0, 4), (1, 4)), (1, 2, 4, 2.0))
    return dict(hidden_in=hidden_in, segment_ids=segment_ids, positions=positions, attn_gain=attn_gain, q_weight=q_weight, k_weight=k_weight, v_weight=v_weight, o_weight=o_weight, mlp_gain=mlp_gain, gate_weight=gate_weight, up_weight=up_weight, down_weight=down_weight, cotangent=cotangent)


EPSILON = 1e-05
THETA_BASE = 100000.0

@jax.custom_vjp
def low(v):
    return lax.optimization_barrier(v.astype(jnp.bfloat16)).astype(jnp.float32)

@jax.custom_vjp
def low_back(v):
    return v

def low_keep(v):
    return (low(v), None)

def low_pass(kept, grad):
    return (grad,)

def back_keep(v):
    return (v, None)

def back_low(kept, grad):
    return (low(grad),)
low.defvjp(low_keep, low_pass)
low_back.defvjp(back_keep, back_low)

def rope_tables(position_values):
    half_dim = HD // 2
    inverse = jnp.power(THETA_BASE, -jnp.arange(half_dim, dtype=jnp.float32) * 2.0 / HD)
    angles = position_values.astype(jnp.float32)[:, None] * inverse[None, :]
    return (jnp.cos(angles), jnp.sin(angles))

def rotate(values, cosine, sine_table):
    token_count = values.shape[0]
    heads_view = values.reshape(token_count, -1, HD)
    half_dim = HD // 2
    first_half = heads_view[..., :half_dim]
    second_half = heads_view[..., half_dim:]
    cos_wide = cosine[:, None, :]
    sin_wide = sine_table[:, None, :]
    turned = jnp.concatenate([first_half * cos_wide - second_half * sin_wide, second_half * cos_wide + first_half * sin_wide], axis=-1)
    return turned.reshape(token_count, -1)

def layer(hidden, gain_first, query_w, key_w, value_w, out_w, gain_second, gate_w, up_w, down_w, seg_ids, position_values):
    highest = lax.Precision.HIGHEST
    pack_len = hidden.shape[0]
    cosine, sine_table = rope_tables(position_values)
    normed_one = low(hidden * lax.rsqrt(lax.optimization_barrier(jnp.mean(hidden * hidden, axis=-1, keepdims=True)) + EPSILON) * gain_first)
    query_rot = low(rotate(low_back(jnp.dot(normed_one, query_w, precision=highest)), cosine, sine_table))
    key_rot = low(rotate(low_back(jnp.dot(normed_one, key_w, precision=highest)), cosine, sine_table))
    value_low = low(low_back(jnp.dot(normed_one, value_w, precision=highest)))
    group_size = HQ // KV
    query_four = query_rot.reshape(pack_len, KV, group_size, HD)
    key_three = key_rot.reshape(pack_len, KV, HD)
    value_three = value_low.reshape(pack_len, KV, HD)
    block_rows = math.gcd(pack_len, 512)
    blocks = pack_len // block_rows
    key_index = jnp.arange(pack_len, dtype=jnp.int32)

    def attend(inputs):
        query_block, seg_block, index_block = inputs
        raw_scores = jnp.einsum('tkgd,skd->tkgs', query_block, key_three, precision=highest)
        scores = low_back(raw_scores * HD ** (-0.5))
        visible = (seg_block[:, None] == seg_ids[None, :]) & (key_index[None, :] <= index_block[:, None])
        scores = jnp.where(visible[:, None, None, :], scores, -1e+30)
        weights = jax.nn.softmax(scores, axis=-1)
        return jnp.einsum('tkgs,skd->tkgd', low(weights), value_three, precision=highest)
    attended = lax.map(jax.checkpoint(attend), (query_four.reshape(blocks, block_rows, KV, group_size, HD), seg_ids.reshape(blocks, block_rows), key_index.reshape(blocks, block_rows)))
    attn_low = low(low_back(attended.reshape(pack_len, HQ * HD)))
    middle = hidden + low_back(jnp.dot(attn_low, out_w.T, precision=highest))
    normed_two = low(middle * lax.rsqrt(lax.optimization_barrier(jnp.mean(middle * middle, axis=-1, keepdims=True)) + EPSILON) * gain_second)
    gate_pre = low_back(jnp.dot(normed_two, gate_w, precision=highest))
    up_pre = low_back(jnp.dot(normed_two, up_w, precision=highest))
    hidden_mlp = low(jax.nn.silu(gate_pre) * up_pre)
    return middle + low_back(jnp.dot(hidden_mlp, down_w.T, precision=highest))

def reference(hidden_in, segment_ids, positions, attn_gain, q_weight, k_weight, v_weight, o_weight, mlp_gain, gate_weight, up_weight, down_weight, cotangent):
    weights_all = tuple((matrix.astype(jnp.float32) for matrix in (attn_gain, q_weight, k_weight, v_weight, o_weight, mlp_gain, gate_weight, up_weight, down_weight)))

    def one_pack(sums_now, items):
        pack_in, pack_segs, pack_pos, pack_cot = items

        def forward(hidden, gain_first, query_w, key_w, value_w, out_w, gain_second, gate_w, up_w, down_w):
            return layer(hidden, gain_first, query_w, key_w, value_w, out_w, gain_second, gate_w, up_w, down_w, pack_segs, pack_pos)
        result, pull_back = jax.vjp(forward, pack_in.astype(jnp.float32), *weights_all)
        grads_all = pull_back(pack_cot.astype(jnp.float32))
        sums_new = tuple((left + right for left, right in zip(sums_now, grads_all[1:])))
        return (sums_new, (result.astype(jnp.bfloat16), grads_all[0].astype(jnp.bfloat16)))
    zeros_all = tuple((jnp.zeros(matrix.shape, jnp.float32) for matrix in weights_all))
    sums_all, outputs = lax.scan(one_pack, zeros_all, (hidden_in, segment_ids, positions, cotangent))
    return (outputs[0], outputs[1], sums_all[0], sums_all[1], sums_all[2], sums_all[3], sums_all[4], sums_all[5], sums_all[6], sums_all[7], sums_all[8])
```

```python
import math

import jax
import jax.numpy as jnp
from jax import lax
from jax.experimental import pallas as pl
from jax.experimental.pallas import tpu as pltpu
from jax.sharding import PartitionSpec as P

HD = 96


EPSILON = 1e-05
THETA_BASE = 100000.0


def mean_scale(values):
    return lax.rsqrt(jnp.mean(values * values, axis=-1, keepdims=True) + EPSILON)


def rope_tables(position_values):
    half_dim = HD // 2
    inverse = jnp.power(THETA_BASE, -jnp.arange(half_dim, dtype=jnp.float32) * 2.0 / HD)
    angles = position_values.astype(jnp.float32)[:, None] * inverse[None, :]
    return (jnp.cos(angles), jnp.sin(angles))


def rotate(values, cosine, sine_table, direction):
    token_count = values.shape[0]
    heads_view = values.reshape(token_count, -1, HD)
    half_dim = HD // 2
    first_half = heads_view[..., :half_dim]
    second_half = heads_view[..., half_dim:]
    cos_wide = cosine[:, None, :]
    sin_wide = direction * sine_table[:, None, :]
    turned = jnp.concatenate(
        [
            first_half * cos_wide - second_half * sin_wide,
            second_half * cos_wide + first_half * sin_wide,
        ],
        axis=-1,
    )
    return turned.reshape(token_count, -1)


def contract_last(left, right):
    return lax.dot_general(
        left, right, (((1,), (1,)), ((), ())), preferred_element_type=jnp.float32
    )


def contract_first(left, right):
    return lax.dot_general(
        left, right, (((0,), (0,)), ((), ())), preferred_element_type=jnp.float32
    )


def norm_back(values, scales, gain_vec, upstream):
    weighted = upstream * gain_vec
    input_part = scales * weighted - values * scales**3 * jnp.mean(
        weighted * values, axis=-1, keepdims=True
    )
    gain_part = jnp.sum(upstream * values * scales, axis=0)
    return (input_part, gain_part)


def general_body(
    hidden_in,
    segment_ids,
    positions,
    attn_gain,
    q_weight,
    k_weight,
    v_weight,
    o_weight,
    mlp_gain,
    gate_weight,
    up_weight,
    down_weight,
    cotangent,
):
    tok_rows = hidden_in.shape[1]
    ctx_count = lax.axis_size("ctx")
    pack_len = tok_rows * ctx_count
    own_start = lax.axis_index("ctx") * tok_rows
    hidden = hidden_in[0].astype(jnp.float32)
    seg_own = segment_ids[0]
    seg_all = lax.all_gather(seg_own, "ctx", axis=0, tiled=True)
    cosine, sine_table = rope_tables(positions[0])
    gain_first, full_query, full_key, full_value, full_out = (
        lax.all_gather(attn_gain, "fsdp", axis=0, tiled=True),
        lax.all_gather(q_weight, "fsdp", axis=0, tiled=True),
        lax.all_gather(k_weight, "fsdp", axis=0, tiled=True),
        lax.all_gather(v_weight, "fsdp", axis=0, tiled=True),
        lax.all_gather(o_weight, "fsdp", axis=0, tiled=True),
    )
    gain_second, full_gate, full_up, full_down = (
        lax.all_gather(mlp_gain, "fsdp", axis=0, tiled=True),
        lax.all_gather(gate_weight, "fsdp", axis=0, tiled=True),
        lax.all_gather(up_weight, "fsdp", axis=0, tiled=True),
        lax.all_gather(down_weight, "fsdp", axis=0, tiled=True),
    )
    scale_one = mean_scale(hidden)
    normed_one = (hidden * scale_one * gain_first.astype(jnp.float32)).astype(jnp.bfloat16)
    query_rot = rotate(
        jnp.dot(normed_one, full_query, preferred_element_type=jnp.float32), cosine, sine_table, 1.0
    ).astype(jnp.bfloat16)
    key_rot = rotate(
        jnp.dot(normed_one, full_key, preferred_element_type=jnp.float32), cosine, sine_table, 1.0
    ).astype(jnp.bfloat16)
    value_low = jnp.dot(normed_one, full_value, preferred_element_type=jnp.float32).astype(
        jnp.bfloat16
    )
    kv_heads = key_rot.shape[1] // HD
    group_size = query_rot.shape[1] // HD // kv_heads
    query_four = query_rot.reshape(tok_rows, kv_heads, group_size, HD)
    query_index = own_start + jnp.arange(tok_rows, dtype=jnp.int32)
    score_scale = HD ** (-0.5)

    def key_mask(key_start, key_count):
        key_index = key_start + jnp.arange(key_count, dtype=jnp.int32)
        key_segs = lax.dynamic_slice_in_dim(seg_all, key_start, key_count)
        return (seg_own[:, None] == key_segs[None, :]) & (
            key_index[None, :] <= query_index[:, None]
        )

    def key_live(key_start, key_count):
        last_seg = lax.dynamic_index_in_dim(seg_all, key_start + key_count - 1, keepdims=False)
        return (key_start <= own_start + tok_rows - 1) & (last_seg >= seg_own[0])

    start_state = (
        jnp.full((tok_rows, kv_heads, group_size), -1e30, jnp.float32),
        jnp.zeros((tok_rows, kv_heads, group_size), jnp.float32),
        jnp.zeros((tok_rows, kv_heads, group_size, HD), jnp.float32),
    )
    key_piece = lax.all_gather(key_rot, "ctx", axis=0, tiled=True)
    value_piece = lax.all_gather(value_low, "ctx", axis=0, tiled=True)
    piece_rows = key_piece.shape[0]
    block_rows = 512

    def one_block(state_in, block_number):
        block_start = block_number * block_rows
        key_block = lax.dynamic_slice_in_dim(key_piece, block_start, block_rows).reshape(
            block_rows, kv_heads, HD
        )
        value_block = lax.dynamic_slice_in_dim(value_piece, block_start, block_rows).reshape(
            block_rows, kv_heads, HD
        )

        def one_live_block(state_old):
            run_max, run_sum, run_acc = state_old
            scores = (
                jnp.einsum(
                    "tkgd,skd->tkgs", query_four, key_block, preferred_element_type=jnp.float32
                )
                * score_scale
            )
            visible = key_mask(block_start, block_rows)[:, None, None, :]
            new_max = jnp.maximum(run_max, jnp.max(jnp.where(visible, scores, -1e30), axis=-1))
            weights = jnp.where(visible, jnp.exp(scores - new_max[..., None]), 0.0)
            fading = jnp.exp(run_max - new_max)
            new_sum = run_sum * fading + jnp.sum(weights, axis=-1)
            new_acc = run_acc * fading[..., None] + jnp.einsum(
                "tkgs,skd->tkgd",
                weights.astype(jnp.bfloat16),
                value_block,
                preferred_element_type=jnp.float32,
            )
            return (new_max, new_sum, new_acc)

        def skip_block(state_old):
            return state_old

        return (
            lax.cond(key_live(block_start, block_rows), one_live_block, skip_block, state_in),
            None,
        )

    state_out, unused = lax.scan(
        one_block, start_state, jnp.arange(piece_rows // block_rows, dtype=jnp.int32)
    )
    run_max, run_sum, run_acc = state_out
    log_total = run_max + jnp.log(run_sum)
    attn_out = run_acc / run_sum[..., None]
    attn_low = attn_out.reshape(tok_rows, -1).astype(jnp.bfloat16)
    attn_proj = lax.psum(contract_last(attn_low, full_out).astype(jnp.bfloat16), "tp").astype(
        jnp.float32
    )
    middle = hidden + attn_proj
    scale_two = mean_scale(middle)
    normed_two = (middle * scale_two * gain_second.astype(jnp.float32)).astype(jnp.bfloat16)
    gate_pre = jnp.dot(normed_two, full_gate, preferred_element_type=jnp.float32)
    up_pre = jnp.dot(normed_two, full_up, preferred_element_type=jnp.float32)
    sigmoid_gate = jax.nn.sigmoid(gate_pre)
    silu_gate = gate_pre * sigmoid_gate
    hidden_mlp = (silu_gate * up_pre).astype(jnp.bfloat16)
    mlp_proj = lax.psum(contract_last(hidden_mlp, full_down).astype(jnp.bfloat16), "tp").astype(
        jnp.float32
    )
    mixed = (middle + mlp_proj).astype(jnp.bfloat16)
    upstream = cotangent[0].astype(jnp.float32)
    grad_out_low = upstream.astype(jnp.bfloat16)
    grad_hidden_mlp = jnp.dot(grad_out_low, full_down, preferred_element_type=jnp.float32)
    down_grad = contract_first(grad_out_low, hidden_mlp)
    grad_gate = (
        grad_hidden_mlp * up_pre * sigmoid_gate * (1.0 + gate_pre * (1.0 - sigmoid_gate))
    ).astype(jnp.bfloat16)
    grad_up = (grad_hidden_mlp * silu_gate).astype(jnp.bfloat16)
    gate_grad = contract_first(normed_two, grad_gate)
    up_grad = contract_first(normed_two, grad_up)
    normed_two_grad = lax.psum(
        (contract_last(grad_gate, full_gate) + contract_last(grad_up, full_up)).astype(
            jnp.bfloat16
        ),
        "tp",
    ).astype(jnp.float32)
    middle_back, gain_second_grad = norm_back(
        middle, scale_two, gain_second.astype(jnp.float32), normed_two_grad
    )
    middle_grad = upstream + middle_back
    proj_low = middle_grad.astype(jnp.bfloat16)
    out_grad = contract_first(proj_low, attn_low)
    grad_attn = jnp.dot(proj_low, full_out, preferred_element_type=jnp.float32).astype(jnp.bfloat16)
    grad_four = grad_attn.reshape(tok_rows, kv_heads, group_size, HD)
    delta_rows = jnp.sum(grad_four.astype(jnp.float32) * attn_out, axis=-1)
    kv_cols = 2 * kv_heads * HD
    query_zero = jnp.zeros((tok_rows, kv_heads, group_size, HD), jnp.float32)
    key_all, value_all = (
        lax.all_gather(key_rot, "ctx", axis=0, tiled=True),
        lax.all_gather(value_low, "ctx", axis=0, tiled=True),
    )
    back_rows = math.gcd(pack_len, 512)
    piece_rows = key_all.shape[0]

    def back_block(acc_in, block_number):
        block_start = block_number * back_rows
        key_block = lax.dynamic_slice_in_dim(key_all, block_start, back_rows).reshape(
            back_rows, kv_heads, HD
        )
        value_block = lax.dynamic_slice_in_dim(value_all, block_start, back_rows).reshape(
            back_rows, kv_heads, HD
        )

        def back_live_block(acc_old):
            scores = (
                jnp.einsum(
                    "tkgd,skd->tkgs", query_four, key_block, preferred_element_type=jnp.float32
                )
                * score_scale
            )
            visible = key_mask(block_start, back_rows)[:, None, None, :]
            weights = jnp.where(visible, jnp.exp(scores - log_total[..., None]), 0.0)
            weights_low = weights.astype(jnp.bfloat16)
            grad_weights = jnp.einsum(
                "tkgd,skd->tkgs", grad_four, value_block, preferred_element_type=jnp.float32
            )
            grad_scores = (weights * (grad_weights - delta_rows[..., None])).astype(jnp.bfloat16)
            acc_new = (
                acc_old
                + jnp.einsum(
                    "tkgs,skd->tkgd", grad_scores, key_block, preferred_element_type=jnp.float32
                )
                * score_scale
            )
            key_part = (
                jnp.einsum(
                    "tkgs,tkgd->skd", grad_scores, query_four, preferred_element_type=jnp.float32
                )
                * score_scale
            )
            value_part = jnp.einsum(
                "tkgs,tkgd->skd", weights_low, grad_four, preferred_element_type=jnp.float32
            )
            return (
                acc_new,
                jnp.concatenate(
                    [key_part.reshape(back_rows, -1), value_part.reshape(back_rows, -1)], axis=1
                ),
            )

        def dead_block(acc_old):
            return (acc_old, jnp.zeros((back_rows, kv_cols), jnp.float32))

        return lax.cond(key_live(block_start, back_rows), back_live_block, dead_block, acc_in)

    acc_out, kv_blocks = lax.scan(
        back_block, query_zero, jnp.arange(piece_rows // back_rows, dtype=jnp.int32)
    )
    kv_pack = kv_blocks.reshape(piece_rows, kv_cols)
    kv_grad = lax.psum_scatter(
        kv_pack.astype(jnp.bfloat16), "ctx", scatter_dimension=0, tiled=True
    ).astype(jnp.float32)
    key_width = key_rot.shape[1]
    grad_query = rotate(acc_out.reshape(tok_rows, -1), cosine, sine_table, -1.0).astype(
        jnp.bfloat16
    )
    grad_key = rotate(kv_grad[:, :key_width], cosine, sine_table, -1.0).astype(jnp.bfloat16)
    grad_value = kv_grad[:, key_width:].astype(jnp.bfloat16)
    query_grad = contract_first(normed_one, grad_query)
    key_grad = contract_first(normed_one, grad_key)
    value_grad = contract_first(normed_one, grad_value)
    normed_one_grad = lax.psum(
        (
            contract_last(grad_query, full_query)
            + contract_last(grad_key, full_key)
            + contract_last(grad_value, full_value)
        ).astype(jnp.bfloat16),
        "tp",
    ).astype(jnp.float32)
    hidden_back, gain_first_grad = norm_back(
        hidden, scale_one, gain_first.astype(jnp.float32), normed_one_grad
    )
    input_grad = (middle_grad + hidden_back).astype(jnp.bfloat16)
    fsdp_summed = (
        lax.psum_scatter(
            gain_first_grad.astype(jnp.bfloat16), "fsdp", scatter_dimension=0, tiled=True
        ).astype(jnp.float32),
        lax.psum_scatter(
            query_grad.astype(jnp.bfloat16), "fsdp", scatter_dimension=0, tiled=True
        ).astype(jnp.float32),
        lax.psum_scatter(
            key_grad.astype(jnp.bfloat16), "fsdp", scatter_dimension=0, tiled=True
        ).astype(jnp.float32),
        lax.psum_scatter(
            value_grad.astype(jnp.bfloat16), "fsdp", scatter_dimension=0, tiled=True
        ).astype(jnp.float32),
        lax.psum_scatter(
            out_grad.astype(jnp.bfloat16), "fsdp", scatter_dimension=0, tiled=True
        ).astype(jnp.float32),
        lax.psum_scatter(
            gain_second_grad.astype(jnp.bfloat16), "fsdp", scatter_dimension=0, tiled=True
        ).astype(jnp.float32),
        lax.psum_scatter(
            gate_grad.astype(jnp.bfloat16), "fsdp", scatter_dimension=0, tiled=True
        ).astype(jnp.float32),
        lax.psum_scatter(
            up_grad.astype(jnp.bfloat16), "fsdp", scatter_dimension=0, tiled=True
        ).astype(jnp.float32),
        lax.psum_scatter(
            down_grad.astype(jnp.bfloat16), "fsdp", scatter_dimension=0, tiled=True
        ).astype(jnp.float32),
    )
    owned = (
        lax.psum(fsdp_summed[0].astype(jnp.bfloat16), "ctx").astype(jnp.float32),
        lax.psum(fsdp_summed[1].astype(jnp.bfloat16), "ctx").astype(jnp.float32),
        lax.psum(fsdp_summed[2].astype(jnp.bfloat16), "ctx").astype(jnp.float32),
        lax.psum(fsdp_summed[3].astype(jnp.bfloat16), "ctx").astype(jnp.float32),
        lax.psum(fsdp_summed[4].astype(jnp.bfloat16), "ctx").astype(jnp.float32),
        lax.psum(fsdp_summed[5].astype(jnp.bfloat16), "ctx").astype(jnp.float32),
        lax.psum(fsdp_summed[6].astype(jnp.bfloat16), "ctx").astype(jnp.float32),
        lax.psum(fsdp_summed[7].astype(jnp.bfloat16), "ctx").astype(jnp.float32),
        lax.psum(fsdp_summed[8].astype(jnp.bfloat16), "ctx").astype(jnp.float32),
    )
    return (
        mixed[None],
        input_grad[None],
        owned[0],
        owned[1],
        owned[2],
        owned[3],
        owned[4],
        owned[5],
        owned[6],
        owned[7],
        owned[8],
    )


BF = jnp.bfloat16
F32 = jnp.float32
BLK = 128
ORDER = ((2, 0), (2, 1), (3, 1), (3, 0), (1, 0), (1, 1), (0, 0), (0, 1))
O_PERM = {
    0: (0, 1, 2, 3, 4, 5, 6, 7),
    1: (3, 2, 1, 0, 6, 7, 4, 5),
    2: (6, 7, 5, 4, 3, 2, 0, 1),
    3: (4, 5, 7, 6, 0, 1, 3, 2),
}
NEG = -1e30
LANES = 128
SCORE = HD**-0.5
LOG2E = 1.4426950408889634
KBLK = 256


def swap_x(a):
    return lax.ppermute(a, "ctx", [(i, i ^ 1) for i in range(4)])


def swap_y(a):
    return lax.ppermute(a, "ctx", [(i, i ^ 2) for i in range(4)])


def swap_d(a):
    return lax.ppermute(a, "ctx", [(i, i ^ 3) for i in range(4)])


def swap_core(a):
    return lax.ppermute(a, "tp", [(0, 1), (1, 0)])


def plane_gather(own):
    half = own.shape[0] // 2
    from_x = swap_x(own)
    from_y = swap_y(own)
    diag_first = swap_y(from_x[:half])
    diag_second = swap_x(from_y[half:])
    return from_x, from_y, diag_first, diag_second


def in_order(own, gathered):
    from_x, from_y, diag_a, diag_b = gathered
    return jnp.concatenate([from_y, diag_b, diag_a, from_x, own], axis=0)


def plane_scatter(part):
    y_one = swap_y(part[BLK : 3 * BLK])
    x_one = swap_x(part[3 * BLK : 5 * BLK])
    x_two = swap_x((part[5 * BLK : 6 * BLK].astype(F32) + y_one[BLK:].astype(F32)).astype(BF))
    y_two = swap_y((part[:BLK].astype(F32) + x_one[:BLK].astype(F32)).astype(BF))
    own_a = part[6 * BLK : 7 * BLK].astype(F32) + x_one[BLK:].astype(F32) + y_two.astype(F32)
    own_b = part[7 * BLK :].astype(F32) + y_one[:BLK].astype(F32) + x_two.astype(F32)
    return jnp.concatenate([own_a, own_b], axis=0)


def dot_nn(left, right):
    return lax.dot_general(left, right, (((1,), (0,)), ((), ())), preferred_element_type=F32)


def dot_nt(left, right):
    return lax.dot_general(left, right, (((1,), (1,)), ((), ())), preferred_element_type=F32)


def dot_tn(left, right):
    return lax.dot_general(left, right, (((0,), (0,)), ((), ())), preferred_element_type=F32)


def vmem(count):
    return [pl.BlockSpec(memory_space=pltpu.VMEM)] * count


def spread_matrix(heads):
    half = HD // 2
    rows = jnp.arange(heads * HD, dtype=jnp.int32)
    target = rows // HD * LANES + rows % HD // half * (LANES // 2) + rows % half
    return (target[:, None] == jnp.arange(heads * LANES, dtype=jnp.int32)[None, :]).astype(BF)


def qkv_kernel(fy, db, da, fx, own, gain, w, cos, sin, n1_ref, q_ref, kv_ref):
    row = 0
    for piece in (fy, db, da, fx, own):
        count = piece.shape[0]
        rows = slice(row, row + count)
        x = piece[...].astype(F32)
        scale = lax.rsqrt(jnp.mean(x * x, axis=-1, keepdims=True) + EPSILON)
        n1 = (x * scale * gain[...]).astype(BF)
        n1_ref[rows, :] = n1
        cos_here, sin_here = cos[rows, :], sin[rows, :]
        out = dot_nn(n1, w[...])
        for head in range(8):
            part = out[:, head * LANES : (head + 1) * LANES]
            if head < 6:
                part = part * cos_here + pltpu.roll(part, LANES // 2, 1) * sin_here
            if head < 4:
                q_ref[head, rows, :] = part.astype(BF)
            else:
                kv_ref[head - 4, rows, :] = part.astype(BF)
        row += count


def block_view(table, index):
    return pl.ds(pl.multiple_of(table[index] * BLK, BLK), BLK)


def attend_kernel(table, q_ref, kv_ref, kvp_ref, start_ref, sel_ref, ot_ref, ob_ref, lse_ref, k_scr, vt_scr):
    i = pl.program_id(0)

    @pl.when(i == 0)
    def _():
        for j in range(8):
            mine, theirs = block_view(table, j), block_view(table, 8 + j)
            rows = slice(j * BLK, (j + 1) * BLK)
            for s in range(2):
                k_scr[s, mine, :] = kv_ref[s, rows, :]
                k_scr[s, theirs, :] = kvp_ref[1 - s, rows, :]
                vt_scr[s, :, mine] = kv_ref[2 + s, rows, :].T
                vt_scr[s, :, theirs] = kvp_ref[3 - s, rows, :].T

    g = table[i]
    first = table[16 + i] // KBLK
    last = (g * BLK + BLK - 1) // KBLK
    lane = lax.broadcasted_iota(jnp.int32, (1, 2 * BLK), 1) % BLK
    q_index = g * BLK + lane
    start = start_ref[0]
    start = jnp.concatenate([start, start], axis=1)
    queries = [jnp.concatenate([q_ref[2 * s], q_ref[2 * s + 1]], axis=0) for s in range(2)]

    def step(kb, state):
        base = pl.multiple_of(kb * KBLK, KBLK)
        k_index = base + lax.broadcasted_iota(jnp.int32, (KBLK, 1), 0)
        visible = (k_index <= q_index) & (k_index >= start)
        new = []
        for s in range(2):
            run_max, run_sum, acc = state[s]
            scores = dot_nt(k_scr[s, pl.ds(base, KBLK), :], queries[s])
            scores = jnp.where(visible, scores, NEG)
            top = jnp.maximum(run_max, jnp.max(scores, axis=0, keepdims=True))
            weights = jnp.exp2((scores - top) * (SCORE * LOG2E))
            fade = jnp.exp2((run_max - top) * (SCORE * LOG2E))
            run_sum = run_sum * fade + jnp.sum(weights, axis=0, keepdims=True)
            acc = acc * fade + dot_nn(vt_scr[s, :, pl.ds(base, KBLK)], weights.astype(BF))
            new.append((top, run_sum, acc))
        return tuple(new)

    one = (
        jnp.full((1, 2 * BLK), NEG, F32),
        jnp.zeros((1, 2 * BLK), F32),
        jnp.zeros((LANES, 2 * BLK), F32),
    )
    state = lax.fori_loop(first, last + 1, step, (one, one))
    heads = []
    for s in range(2):
        top, total, acc = state[s]
        out_t = acc / total
        ot_ref[s, 0] = out_t
        lse_ref[s, 0] = top * (SCORE * LOG2E) + jnp.log2(total)
        out = out_t.T.astype(BF)
        heads += [out[:BLK], out[BLK:]]
    ob_ref[...] = dot_nt(jnp.concatenate(heads, axis=1), sel_ref[...]).astype(BF)


def attend_back_kernel(
    table, q_ref, kv_ref, kvp_ref, start_ref, sel_ref, cos_ref, sin_ref, ot_ref, lse_ref, do_ref,
    dq_ref, dkv_ref, dkvp_ref, k_scr, kt_scr, v_scr, dk_scr, dv_scr,
):
    i = pl.program_id(0)

    @pl.when(i == 0)
    def _():
        dk_scr[...] = jnp.zeros_like(dk_scr)
        dv_scr[...] = jnp.zeros_like(dv_scr)
        for j in range(8):
            mine, theirs = block_view(table, j), block_view(table, 8 + j)
            rows = slice(j * BLK, (j + 1) * BLK)
            for s in range(2):
                k_own, k_other = kv_ref[s, rows, :], kvp_ref[1 - s, rows, :]
                k_scr[s, mine, :] = k_own
                k_scr[s, theirs, :] = k_other
                kt_scr[s, :, mine] = k_own.T
                kt_scr[s, :, theirs] = k_other.T
                v_scr[s, mine, :] = kv_ref[2 + s, rows, :]
                v_scr[s, theirs, :] = kvp_ref[3 - s, rows, :]

    g = table[i]
    first = table[16 + i] // KBLK
    last = (g * BLK + BLK - 1) // KBLK
    lane = lax.broadcasted_iota(jnp.int32, (1, 2 * BLK), 1) % BLK
    q_index = g * BLK + lane
    start = start_ref[0]
    start = jnp.concatenate([start, start], axis=1)
    grads_wide = dot_nn(do_ref[...], sel_ref[...])
    queries, grads, deltas, lses = [], [], [], []
    for s in range(2):
        queries.append(jnp.concatenate([q_ref[2 * s], q_ref[2 * s + 1]], axis=0))
        lo = 2 * s * LANES
        wide = jnp.concatenate([grads_wide[:, lo : lo + LANES], grads_wide[:, lo + LANES : lo + 2 * LANES]], axis=0)
        grads.append(wide.astype(BF))
        deltas.append(jnp.sum(wide.T * ot_ref[s, 0], axis=0, keepdims=True))
        lses.append(lse_ref[s, 0])

    def step(kb, state):
        base = pl.multiple_of(kb * KBLK, KBLK)
        here = pl.ds(base, KBLK)
        k_index = base + lax.broadcasted_iota(jnp.int32, (KBLK, 1), 0)
        visible = (k_index <= q_index) & (k_index >= start)
        new = []
        for s in range(2):
            scores = dot_nt(k_scr[s, here, :], queries[s])
            weights = jnp.where(visible, jnp.exp2(scores * (SCORE * LOG2E) - lses[s]), 0.0)
            d_weights = dot_nt(v_scr[s, here, :], grads[s])
            d_scores = (weights * (d_weights - deltas[s])).astype(BF)
            dv_scr[s, here, :] += dot_nn(weights.astype(BF), grads[s])
            dk_scr[s, here, :] += dot_nn(d_scores, queries[s])
            new.append(state[s] + dot_nn(kt_scr[s, :, here], d_scores))
        return tuple(new)

    zero = jnp.zeros((LANES, 2 * BLK), F32)
    state = lax.fori_loop(first, last + 1, step, (zero, zero))
    cos, sin = cos_ref[...], sin_ref[...]
    for s in range(2):
        d_q = state[s].T * SCORE
        for h in range(2):
            part = d_q[h * BLK : (h + 1) * BLK]
            part = part * cos - pltpu.roll(part, LANES // 2, 1) * sin
            dq_ref[:, (2 * s + h) * LANES : (2 * s + h + 1) * LANES] = part.astype(BF)

    @pl.when(i == pl.num_programs(0) - 1)
    def _():
        for j in range(8):
            mine, theirs = block_view(table, j), block_view(table, 8 + j)
            rows = slice(j * BLK, (j + 1) * BLK)
            for s in range(2):
                for which, scr, scale in ((0, dk_scr, SCORE), (2, dv_scr, 1.0)):
                    to = (which + s) * LANES
                    dkv_ref[rows, to : to + LANES] = scr[s, mine, :] * scale
                    to = (which + 1 - s) * LANES
                    dkvp_ref[rows, to : to + LANES] = (scr[s, theirs, :] * scale).astype(BF)


def middle_kernel(oo, ox, oy, od1, od2, ow, fy, db, da, fx, own, gain, n2_ref, h2_ref):
    def heads_of(e, block):
        if e < 3:
            ref = (oo, ox, oy)[e]
            return ref[block * BLK : (block + 1) * BLK, :]
        ref = od1 if block < 4 else od2
        return ref[block % 4 * BLK : (block % 4 + 1) * BLK, :]

    for pair in range(4):
        both = (2 * pair, 2 * pair + 1)
        heads = jnp.concatenate(
            [jnp.concatenate([heads_of(e, O_PERM[e][b]) for e in range(4)], axis=1) for b in both], axis=0
        )
        if pair == 0:
            x = fy[...]
        elif pair == 1:
            x = jnp.concatenate([db[...], da[...]], axis=0)
        else:
            x = (fx if pair == 2 else own)[...]
        h2 = x.astype(F32) + dot_nt(heads, ow[...])
        scale = lax.rsqrt(jnp.mean(h2 * h2, axis=-1, keepdims=True) + EPSILON)
        n2_ref[pair * 2 * BLK : (pair + 1) * 2 * BLK, :] = (h2 * scale * gain[...]).astype(BF)
        if pair == 3:
            h2_ref[...] = h2


def mlp_kernel(n2, gy, wg, wu, wd, hid_ref, dg_ref, du_ref):
    gate = dot_nn(n2[...], wg[...])
    up = dot_nn(n2[...], wu[...])
    d_hid = dot_nn(gy[...], wd[...])
    sig = jax.nn.sigmoid(gate)
    silu = gate * sig
    hid_ref[...] = (silu * up).astype(BF)
    du_ref[...] = (d_hid * silu).astype(BF)
    dg_ref[...] = (d_hid * up * sig * (1.0 + gate * (1.0 - sig))).astype(BF)


def mlp_half(n2, gy, gate_up, down, tile=256):
    rows, width = n2.shape
    cols = down.shape[1]
    steps = cols // tile
    whole = pl.BlockSpec((rows, width), lambda j: (0, 0), pipeline_mode=pl.Buffered(1))
    out = pl.BlockSpec((rows, tile), lambda j: (0, j))
    return pl.pallas_call(
        mlp_kernel,
        grid=(steps,),
        in_specs=[
            whole,
            whole,
            pl.BlockSpec((width, tile), lambda j: (0, j)),
            pl.BlockSpec((width, tile), lambda j: (0, j + steps)),
            pl.BlockSpec((width, tile), lambda j: (0, j)),
        ],
        out_specs=[out] * 3,
        out_shape=[jax.ShapeDtypeStruct((rows, cols), BF)] * 3,
        cost_estimate=pl.CostEstimate(
            flops=6 * rows * width * cols, bytes_accessed=4 * rows * width + 6 * width * cols, transcendentals=rows * cols
        ),
        name="mlp",
    )(n2, gy, gate_up, gate_up, down)


def sum_dots(terms, name, tile=256):
    rows = terms[0][0].shape[0]
    depth = terms[0][0].shape[1]
    out_cols = terms[0][1].shape[0]

    def kernel(*refs):
        half = len(terms)
        total = dot_nt(refs[0][...], refs[half][...])
        for n in range(1, half):
            total = total + dot_nt(refs[n][...], refs[half + n][...])
        refs[-1][...] = total.astype(BF)

    def right_spec(block):
        return pl.BlockSpec((out_cols, depth), lambda i: (0, block), pipeline_mode=pl.Buffered(1))

    return pl.pallas_call(
        kernel,
        grid=(rows // tile,),
        in_specs=[pl.BlockSpec((tile, depth), lambda i: (i, 0))] * len(terms) + [right_spec(t[2]) for t in terms],
        out_specs=pl.BlockSpec((tile, out_cols), lambda i: (i, 0)),
        out_shape=jax.ShapeDtypeStruct((rows, out_cols), BF),
        cost_estimate=pl.CostEstimate(
            flops=2 * rows * depth * out_cols * len(terms),
            bytes_accessed=2 * (rows * depth + out_cols * depth) * len(terms) + 2 * rows * out_cols,
            transcendentals=0,
        ),
        name=name,
    )(*[t[0] for t in terms], *[t[1] for t in terms])


def project_back_kernel(dq, dkv, dkvp, cos, sin, w, dkv_ref, out_ref):
    both = dkv[...] + dkvp[...].astype(F32)
    parts = []
    for head in range(4):
        part = both[:, head * LANES : (head + 1) * LANES]
        if head < 2:
            part = part * cos[...] - pltpu.roll(part, LANES // 2, 1) * sin[...]
        parts.append(part.astype(BF))
    low = jnp.concatenate(parts, axis=1)
    dkv_ref[...] = low
    half = w.shape[1] // 2
    out_ref[...] = (dot_nt(dq[...], w[:, :half]) + dot_nt(low, w[:, half:])).astype(BF)


def from_relative(own, from_x, from_y, from_d, x_bit, y_bit):
    low = jnp.where(x_bit, jnp.concatenate([from_x, own], 1), jnp.concatenate([own, from_x], 1))
    high = jnp.where(x_bit, jnp.concatenate([from_d, from_y], 1), jnp.concatenate([from_y, from_d], 1))
    return jnp.where(y_bit, jnp.concatenate([high, low], 1), jnp.concatenate([low, high], 1))


def plane_body(
    hidden_in,
    segment_ids,
    positions,
    attn_gain,
    q_weight,
    k_weight,
    v_weight,
    o_weight,
    mlp_gain,
    gate_weight,
    up_weight,
    down_weight,
    cotangent,
):
    c = lax.axis_index("ctx")
    k = lax.axis_index("tp")
    x_bit, y_bit = (c & 1) == 1, (c & 2) == 2
    width = hidden_in.shape[2]
    fsdp = lax.axis_size("fsdp")

    def own_rows(a):
        return jnp.concatenate(
            [lax.dynamic_slice_in_dim(a, k * BLK, BLK), lax.dynamic_slice_in_dim(a, 3 * BLK - k * BLK, BLK)], axis=0
        )

    def cols(w, parts=4):
        size = w.shape[1] // parts
        return lax.dynamic_slice_in_dim(w, c * size, size, axis=1)

    pos_own = own_rows(positions[0])[:, None].reshape(2, BLK)
    x_own = own_rows(hidden_in[0])
    x_from = plane_gather(x_own)
    pos_x, pos_y, pos_d = swap_x(pos_own), swap_y(pos_own), swap_d(pos_own)
    pos = jnp.stack([(pos_own, pos_x, pos_y, pos_d)[e][ab] for e, ab in ORDER])

    qkv_own = lax.all_gather(jnp.concatenate([cols(q_weight), cols(k_weight), cols(v_weight)], 1), "fsdp", tiled=True)
    gains = lax.all_gather(jnp.stack([attn_gain, mlp_gain], 0)[None], "fsdp", axis=0, tiled=True)
    gains = gains.transpose(1, 0, 2).reshape(2, width).astype(F32)
    q_cols = o_weight.shape[1] // 4
    o_blocks = [o_weight[:, j * q_cols : (j + 1) * q_cols] for j in range(4)]
    o_pairs = [
        jnp.where(x_bit, jnp.concatenate([b, a], 1), jnp.concatenate([a, b], 1))
        for a, b in ((o_blocks[0], o_blocks[1]), (o_blocks[2], o_blocks[3]))
    ]
    o_rel = jnp.where(y_bit, jnp.concatenate(o_pairs[::-1], 1), jnp.concatenate(o_pairs, 1))
    o_own = lax.all_gather(o_rel, "fsdp", tiled=True)
    gu_own = lax.all_gather(jnp.concatenate([cols(gate_weight), cols(up_weight)], 1), "fsdp", tiled=True)
    d_own = lax.all_gather(cols(down_weight), "fsdp", tiled=True)
    qkv_par = swap_core(qkv_own)
    o_par = swap_core(o_own)
    gu_par = swap_core(gu_own)
    d_par = swap_core(d_own)

    kv_cols = q_cols // 2
    spread_q, spread_k = spread_matrix(4), spread_matrix(2)
    spread_all = []
    for s in range(2):
        block = jnp.zeros((2 * q_cols, 8 * LANES), BF)
        block = block.at[:q_cols, : 4 * LANES].set(spread_q[s * q_cols : (s + 1) * q_cols])
        block = block.at[q_cols : q_cols + kv_cols, 4 * LANES : 6 * LANES].set(spread_k[s * kv_cols : (s + 1) * kv_cols])
        block = block.at[q_cols + kv_cols :, 6 * LANES :].set(spread_k[s * kv_cols : (s + 1) * kv_cols])
        spread_all.append(block)
    w_pad = (dot_nn(qkv_own, spread_all[0]) + dot_nn(qkv_par, spread_all[1])).astype(BF)
    o_full = jnp.concatenate(
        [(o_own, o_par)[s][:, e * q_cols : (e + 1) * q_cols] for e in range(4) for s in range(2)], axis=1
    )

    half_dim = HD // 2
    lane = jnp.arange(LANES, dtype=jnp.int32)
    inner = lane % (LANES // 2)
    inverse = jnp.power(THETA_BASE, -inner.astype(F32) * 2.0 / HD)
    inverse = jnp.where(inner < half_dim, inverse, 0.0)
    angles = pos.reshape(-1).astype(F32)[:, None] * inverse[None, :]
    cosine = jnp.cos(angles)
    sine = jnp.sin(angles) * jnp.where(lane < LANES // 2, -1.0, 1.0)[None, :]

    rows = 8 * BLK
    pieces = (x_from[1], x_from[3], x_from[2], x_from[0], x_own)
    n1, q_all, kv_all = pl.pallas_call(
        qkv_kernel,
        in_specs=vmem(9),
        out_specs=vmem(3),
        out_shape=[
            jax.ShapeDtypeStruct((rows, width), BF),
            jax.ShapeDtypeStruct((4, rows, LANES), BF),
            jax.ShapeDtypeStruct((4, rows, LANES), BF),
        ],
        cost_estimate=pl.CostEstimate(flops=2 * rows * width * 1024, bytes_accessed=12 << 20, transcendentals=0),
        name="qkv",
    )(*pieces, gains[:1], w_pad, cosine, sine)
    kv_par = swap_core(kv_all)

    chip = jnp.stack([c ^ e for e, _ in ORDER])
    mine = jnp.stack([k if ab == 0 else 3 - k for _, ab in ORDER])
    theirs = jnp.stack([1 - k if ab == 0 else 2 + k for _, ab in ORDER])
    g_mine = chip * 4 + mine
    starts = g_mine[:, None] * BLK + jnp.arange(BLK, dtype=jnp.int32)[None, :] - pos
    table = jnp.concatenate([g_mine, chip * 4 + theirs, starts[:, 0]]).astype(jnp.int32)
    starts = starts[:, None, :]
    pack_len = 16 * BLK

    def const(shape):
        return pl.BlockSpec(shape, lambda i, t: (0,) * len(shape), pipeline_mode=pl.Buffered(1))

    head_rows = pl.BlockSpec((4, BLK, LANES), lambda i, t: (0, i, 0))
    start_spec = pl.BlockSpec((1, 1, BLK), lambda i, t: (i, 0, 0))
    ot_spec = pl.BlockSpec((2, 1, LANES, 2 * BLK), lambda i, t: (0, i, 0, 0))
    lse_spec = pl.BlockSpec((2, 1, 1, 2 * BLK), lambda i, t: (0, i, 0, 0))
    heads_spec = pl.BlockSpec((BLK, 4 * HD), lambda i, t: (i, 0))
    o_t, o_low, lse = pl.pallas_call(
        attend_kernel,
        grid_spec=pltpu.PrefetchScalarGridSpec(
            num_scalar_prefetch=1,
            grid=(8,),
            in_specs=[
                head_rows,
                const((4, rows, LANES)),
                const((4, rows, LANES)),
                start_spec,
                const((4 * HD, 4 * LANES)),
            ],
            out_specs=[ot_spec, heads_spec, lse_spec],
            scratch_shapes=[pltpu.VMEM((2, pack_len, LANES), BF), pltpu.VMEM((2, LANES, pack_len), BF)],
        ),
        out_shape=[
            jax.ShapeDtypeStruct((2, 8, LANES, 2 * BLK), F32),
            jax.ShapeDtypeStruct((rows, 4 * HD), BF),
            jax.ShapeDtypeStruct((2, 8, 1, 2 * BLK), F32),
        ],
        cost_estimate=pl.CostEstimate(flops=4 << 30, bytes_accessed=8 << 20, transcendentals=4 << 20),
        name="attend",
    )(table, q_all, kv_all, kv_par, starts, spread_q)

    o_from = plane_gather(o_low)
    n2, h2_own = pl.pallas_call(
        middle_kernel,
        in_specs=vmem(12),
        out_specs=vmem(2),
        out_shape=[jax.ShapeDtypeStruct((rows, width), BF), jax.ShapeDtypeStruct((2 * BLK, width), F32)],
        cost_estimate=pl.CostEstimate(flops=2 * rows * width * width, bytes_accessed=18 << 20, transcendentals=0),
        name="middle",
    )(o_low, o_from[0], o_from[1], o_from[2], o_from[3], o_full, *pieces, gains[1:])

    gy_own = own_rows(cotangent[0])
    gy = in_order(gy_own, plane_gather(gy_own))

    hid_a, dg_a, du_a = mlp_half(n2, gy, gu_own, d_own)
    hid_b, dg_b, du_b = mlp_half(n2, gy, gu_par, d_par)
    dn2_part = sum_dots([(dg_a, gu_own, 0), (du_a, gu_own, 1), (dg_b, gu_par, 0), (du_b, gu_par, 1)], "dn2")
    dn2 = plane_scatter(dn2_part)

    gain_two = gains[1:]
    scale_two = lax.rsqrt(jnp.mean(h2_own * h2_own, axis=-1, keepdims=True) + EPSILON)
    weighted = dn2 * gain_two
    dh2 = (
        gy_own.astype(F32)
        + scale_two * weighted
        - h2_own * scale_two**3 * jnp.mean(weighted * h2_own, axis=-1, keepdims=True)
    )
    gm_own = dh2.astype(BF)
    gm = in_order(gm_own, plane_gather(gm_own))
    grad_heads = dot_nn(gm, o_full[:, : 2 * q_cols]).astype(BF)

    tab_rows = pl.BlockSpec((BLK, LANES), lambda i, t: (i, 0))
    dq, dkv_own, dkv_send = pl.pallas_call(
        attend_back_kernel,
        grid_spec=pltpu.PrefetchScalarGridSpec(
            num_scalar_prefetch=1,
            grid=(8,),
            in_specs=[
                head_rows,
                const((4, rows, LANES)),
                const((4, rows, LANES)),
                start_spec,
                const((4 * HD, 4 * LANES)),
                tab_rows,
                tab_rows,
                ot_spec,
                lse_spec,
                heads_spec,
            ],
            out_specs=[
                pl.BlockSpec((BLK, 4 * LANES), lambda i, t: (i, 0)),
                const((rows, 4 * LANES)),
                const((rows, 4 * LANES)),
            ],
            scratch_shapes=[
                pltpu.VMEM((2, pack_len, LANES), BF),
                pltpu.VMEM((2, LANES, pack_len), BF),
                pltpu.VMEM((2, pack_len, LANES), BF),
                pltpu.VMEM((2, pack_len, LANES), F32),
                pltpu.VMEM((2, pack_len, LANES), F32),
            ],
        ),
        out_shape=[
            jax.ShapeDtypeStruct((rows, 4 * LANES), BF),
            jax.ShapeDtypeStruct((rows, 4 * LANES), F32),
            jax.ShapeDtypeStruct((rows, 4 * LANES), BF),
        ],
        cost_estimate=pl.CostEstimate(flops=10 << 30, bytes_accessed=14 << 20, transcendentals=4 << 20),
        name="attend_back",
    )(table, q_all, kv_all, kv_par, starts, spread_q, cosine, sine, o_t, lse, grad_heads)
    dkv_par = swap_core(dkv_send)
    row_spec = pl.BlockSpec((2 * BLK, 4 * LANES), lambda i: (i, 0))
    tab_spec = pl.BlockSpec((2 * BLK, LANES), lambda i: (i, 0))
    dkv, dn1_part = pl.pallas_call(
        project_back_kernel,
        grid=(4,),
        in_specs=[
            row_spec,
            row_spec,
            row_spec,
            tab_spec,
            tab_spec,
            pl.BlockSpec((width, 8 * LANES), lambda i: (0, 0), pipeline_mode=pl.Buffered(1)),
        ],
        out_specs=[row_spec, pl.BlockSpec((2 * BLK, width), lambda i: (i, 0))],
        out_shape=[jax.ShapeDtypeStruct((rows, 4 * LANES), BF), jax.ShapeDtypeStruct((rows, width), BF)],
        cost_estimate=pl.CostEstimate(flops=2 * rows * width * 1024, bytes_accessed=12 << 20, transcendentals=0),
        name="project_back",
    )(dq, dkv_own, dkv_par, cosine, sine, w_pad)

    dn1 = plane_scatter(dn1_part)
    hidden = x_own.astype(F32)
    scale_one = lax.rsqrt(jnp.mean(hidden * hidden, axis=-1, keepdims=True) + EPSILON)
    weighted = dn1 * gains[:1]
    input_own = (
        dh2
        + scale_one * weighted
        - hidden * scale_one**3 * jnp.mean(weighted * hidden, axis=-1, keepdims=True)
    ).astype(BF)

    def all_rows(own):
        other = swap_core(own)
        a0, b0 = own[:BLK], own[BLK:]
        a1, b1 = other[:BLK], other[BLK:]
        return jnp.where(k == 0, jnp.concatenate([a0, a1, b1, b0], 0), jnp.concatenate([a1, a0, b0, b1], 0))

    input_grad = all_rows(input_own)
    mixed_part = sum_dots([(hid_a, d_own, 0), (hid_b, d_par, 0)], "mixed")
    mixed = all_rows((h2_own + plane_scatter(mixed_part)).astype(BF))

    d_qkv = jnp.concatenate([dq, dkv], axis=1)
    d_qkv_own = dot_nt(d_qkv, spread_all[0]).astype(BF)
    d_qkv_par = dot_nt(d_qkv, spread_all[1]).astype(BF)

    def halves(left, own, par):
        got = swap_core(dot_tn(left, par).astype(BF))
        return (dot_tn(left, own) + got.astype(F32)).astype(BF)

    down_part = halves(gy, hid_a, hid_b)
    gate_part = halves(n2, dg_a, dg_b)
    up_part = halves(n2, du_a, du_b)
    o_part = halves(gm, o_low[:, :q_cols], o_low[:, q_cols:])
    qkv_part = halves(n1, d_qkv_own, d_qkv_par)

    def gain_rows(part, normed):
        one = jnp.sum(part.astype(F32) * normed.astype(F32), axis=0).astype(BF)
        one = (one.astype(F32) + swap_core(one).astype(F32)).astype(BF)
        return one.reshape(fsdp, 1, width // fsdp)

    def slab(grads, gain):
        grads = grads.reshape(fsdp, width // fsdp, grads.shape[1])
        extra = jnp.pad(gain, ((0, 0), (0, 15), (0, grads.shape[2] - gain.shape[2])))
        whole = jnp.concatenate([grads, extra], axis=1)
        return whole.reshape(-1, whole.shape[2])

    def owned(part):
        own = lax.psum_scatter(part, "fsdp", scatter_dimension=0, tiled=True)
        from_x, from_y = swap_x(own), swap_y(own)
        half = own.shape[0] // 2
        from_d = jnp.concatenate([swap_y(from_x[:half]), swap_x(from_y[half:])], axis=0)
        return own, from_x, from_y, from_d

    own_width = width // fsdp

    def spread_out(gathered, lo, hi):
        return from_relative(*[p[:own_width, lo:hi].astype(F32) for p in gathered], x_bit, y_bit)

    def gain_of(gathered, gain):
        total = sum(p[own_width, :own_width].astype(F32) for p in gathered)
        return total / gain.astype(F32)

    down_all = owned(down_part)
    gu_all = owned(slab(jnp.concatenate([gate_part, up_part], 1), gain_rows(dn2_part, n2)))
    o_all = owned(o_part)
    qkv_all = owned(slab(qkv_part, gain_rows(dn1_part, n1)))
    ff_cols = down_part.shape[1]
    return (
        mixed[None],
        input_grad[None],
        gain_of(qkv_all, attn_gain),
        spread_out(qkv_all, 0, q_cols),
        spread_out(qkv_all, q_cols, q_cols + kv_cols),
        spread_out(qkv_all, q_cols + kv_cols, 2 * q_cols),
        spread_out(o_all, 0, q_cols),
        gain_of(gu_all, mlp_gain),
        spread_out(gu_all, 0, ff_cols),
        spread_out(gu_all, ff_cols, 2 * ff_cols),
        spread_out(down_all, 0, ff_cols),
    )


def solution(mesh):
    return jax.shard_map(
        plane_body if mesh.shape["ctx"] == 4 else general_body,
        mesh=mesh,
        in_specs=(
            P("fsdp", "ctx", None),
            P("fsdp", "ctx"),
            P("fsdp", "ctx"),
            P("fsdp"),
            P("fsdp", "tp"),
            P("fsdp", "tp"),
            P("fsdp", "tp"),
            P("fsdp", "tp"),
            P("fsdp"),
            P("fsdp", "tp"),
            P("fsdp", "tp"),
            P("fsdp", "tp"),
            P("fsdp", "ctx", None),
        ),
        out_specs=(
            P("fsdp", "ctx", None),
            P("fsdp", "ctx", None),
            P("fsdp"),
            P("fsdp", "tp"),
            P("fsdp", "tp"),
            P("fsdp", "tp"),
            P("fsdp", "tp"),
            P("fsdp"),
            P("fsdp", "tp"),
            P("fsdp", "tp"),
            P("fsdp", "tp"),
        ),
        check_vma=False,
    )
```
